128 devices in a mesh: walker: 16 (over x, y_hi, core), prow: 2 (over y_lo), pcol: 4 (over z).
Axes of the slice: x: 4, y: 4 (y_hi: 2, y_lo: 2; y = y_hi * 2 + y_lo), z: 4, core: 2. Of those that a mesh axis runs over, the one named last changes fastest.
Arguments:
- o_rows: bfloat16 [32768, 2048], P('walker', ('prow', 'pcol')), may hold values from -21 to 21
- o_cols: bfloat16 [32768, 4096], P('walker', ('pcol', 'prow')), may hold values from -48 to 48
- grad_energy: bfloat16 [32768, 4096], P('walker', ('pcol', 'prow')), may hold values from -8 to 8
- energy: float32 [32768], P('walker'), may hold values from -5 to 1
Outputs:
- hamil: float32 [2048, 4096], P(('prow', 'walker'), 'pcol')
- correlation: float32 [2048, 4096], P(('prow', 'walker'), 'pcol')
The draws below stay inside these ranges and needn't reach their ends.
All inputs are finite; a program needn't handle non-finite values.
Results may differ from the reference program's by a relative error of at most 0.008.
Values may be sent and summed in bfloat16 or wider, within the bound.
A program may use at most 128 MiB of HBM per device.

```python
import jax
import jax.numpy as jnp
from jax import lax

SAMPLES = 32768
ROWS = 2048
NCOL = 4096


def noise_field(key, shape):
    return jnp.clip(jax.random.normal(key, shape, jnp.float32), -4.0, 4.0)


def sample_scale():
    return 0.5 + jnp.arange(SAMPLES, dtype=jnp.float32) / SAMPLES


def offsets(key, count):
    return jax.random.uniform(key, (count,), jnp.float32, -2.0, 2.0)


def col_scales(key, count):
    return jnp.exp(jax.random.uniform(key, (count,), jnp.float32, jnp.log(0.3), jnp.log(3.0)))


def shared_base(key):
    return noise_field(jax.random.fold_in(key, 1), (SAMPLES, ROWS))


def tiled_base(key):
    return jnp.tile(shared_base(key), (1, NCOL // ROWS))


def draw_o_rows(key, part):
    base = shared_base(key)
    shift = offsets(jax.random.fold_in(key, 2), ROWS)
    spread = col_scales(jax.random.fold_in(key, 3), ROWS)
    values = sample_scale()[:, None] * (shift + spread * base)
    return values.astype(jnp.bfloat16)


def draw_o_cols(key, part):
    tiled = tiled_base(key)
    mixing = jax.random.uniform(jax.random.fold_in(key, 4), (NCOL,), jnp.float32, 0.5, 1.5)
    own_part = noise_field(jax.random.fold_in(key, 5), (SAMPLES, NCOL))
    spread = col_scales(jax.random.fold_in(key, 6), NCOL)
    shift = offsets(jax.random.fold_in(key, 7), NCOL)
    values = sample_scale()[:, None] * (shift + spread * (mixing * tiled + own_part))
    return values.astype(jnp.bfloat16)


def draw_grad_energy(key, part):
    tiled = tiled_base(key)
    factor = jax.random.uniform(jax.random.fold_in(key, 8), (NCOL,), jnp.float32, 0.5, 1.5)
    extra = noise_field(jax.random.fold_in(key, 9), (SAMPLES, NCOL))
    return (factor * tiled + 0.5 * extra).astype(jnp.bfloat16)


def draw_energy(key, part):
    extra = noise_field(jax.random.fold_in(key, 10), (SAMPLES,))
    return -(0.5 + 1.5 * sample_scale()) + 0.5 * extra


def setup_inputs(seed: int = 0) -> dict:
    key_list = jax.random.split(jax.random.key(seed), 5)
    o_rows = draw_o_rows(jax.random.fold_in(key_list[4], 71), 0)
    o_cols = draw_o_cols(jax.random.fold_in(key_list[4], 71), 0)
    grad_energy = draw_grad_energy(jax.random.fold_in(key_list[4], 71), 0)
    energy = draw_energy(jax.random.fold_in(key_list[4], 71), 0)
    return dict(o_rows=o_rows, o_cols=o_cols, grad_energy=grad_energy, energy=energy)


def reference(o_rows, o_cols, grad_energy, energy):
    row_mean = jnp.sum(o_rows.astype(jnp.float32), axis=0) / SAMPLES
    col_mean = jnp.sum(o_cols.astype(jnp.float32), axis=0) / SAMPLES
    d_rows = (o_rows.astype(jnp.float32) - row_mean).astype(jnp.bfloat16)
    d_cols = (o_cols.astype(jnp.float32) - col_mean).astype(jnp.bfloat16)
    weighted = (energy[:, None] * d_cols.astype(jnp.float32) + grad_energy.astype(jnp.float32)).astype(jnp.bfloat16)
    dims = (((0,), (0,)), ((), ()))
    correlation = lax.dot_general(d_rows, d_cols, dims, preferred_element_type=jnp.float32) / SAMPLES
    hamil = lax.dot_general(d_rows, weighted, dims, preferred_element_type=jnp.float32) / SAMPLES
    return hamil, correlation
```

```python
import functools

import jax
import jax.numpy as jnp
from jax import lax
from jax.experimental import pallas as pl
from jax.experimental.pallas import tpu as pltpu
from jax.sharding import PartitionSpec as P

MESH = pl.DeviceIdType.MESH
F32 = jnp.float32
BF16 = jnp.bfloat16

PIECE = 512


def kernel(total, o_hbm, c_hbm, g_hbm, e_hbm, ham_ref, cor_ref,
           rows, cols, grads, en, rhs, pacc, stat, stat_x, rmean,
           core_out, core_in, x_out, x_in, x_acc, y_out, y_in, y_keep,
           load_sem, rs_send, rs_recv, st_send, st_recv, rm_send, rm_recv,
           c_send, c_recv, x_send, x_recv, y_send, y_recv):
    w = lax.axis_index("walker")
    p = lax.axis_index("prow")
    q = lax.axis_index("pcol")
    x, yh, c = w // 4, (w // 2) % 2, w % 2

    def walker(xx, yy, cc):
        return xx * 4 + yy * 2 + cc

    partner = (walker(x, yh, 1 - c), p, q)
    xs = [(walker((x + k) % 4, yh, c), p, q) for k in (1, 2, 3)]
    far = (walker(x, 1 - yh, c), p, q)
    near = (w, 1 - p, q)
    diag = (walker(x, 1 - yh, c), 1 - p, q)
    up = (w, p, (q + 1) % 4)
    down = (w, p, (q + 3) % 4)
    peers = [partner, *xs, far, near, diag, up, down]

    loads = [
        pltpu.make_async_copy(o_hbm, rows.at[0], load_sem.at[0]),
        pltpu.make_async_copy(c_hbm, cols, load_sem.at[1]),
        pltpu.make_async_copy(e_hbm, en, load_sem.at[2]),
        pltpu.make_async_copy(g_hbm, grads, load_sem.at[3]),
    ]
    for load in loads:
        load.start()

    barrier = pltpu.get_barrier_semaphore()
    for peer in peers:
        pl.semaphore_signal(barrier, inc=1, device_id=peer, device_id_type=MESH)
    pl.semaphore_wait(barrier, len(peers))

    started = []

    def start(src, dst, send, recv, device):
        copy = pltpu.make_async_remote_copy(
            src_ref=src, dst_ref=dst, send_sem=send, recv_sem=recv,
            device_id=device, device_id_type=MESH)
        copy.start()
        started.append(copy)

    def arrived(dst, recv):
        pltpu.make_async_remote_copy(
            src_ref=dst, dst_ref=dst, send_sem=recv, recv_sem=recv,
            device_id=near, device_id_type=MESH).wait_recv()

    counter = [0]

    def piece_of(slot, i):
        if slot == 0:
            return o_hbm.at[pl.ds(i * PIECE, PIECE)]
        return rows.at[slot, pl.ds(i * PIECE, PIECE)]

    def send_piece(way, dy, dz, i):
        device, ty, tz = {
            "up": (up, dy, (dz + 3) % 4),
            "down": (down, dy, (dz + 1) % 4),
            "across": (near, 1 - dy, dz),
        }[way]
        target = ty * 4 + tz
        n = counter[0]
        counter[0] += 1
        start(piece_of(dy * 4 + dz, i), rows.at[target, pl.ds(i * PIECE, PIECE)],
              rs_send.at[n], rs_recv.at[target, i], device)

    def piece_in(dy, dz, i):
        slot = dy * 4 + dz
        arrived(rows.at[slot, pl.ds(i * PIECE, PIECE)], rs_recv.at[slot, i])

    send_piece("up", 0, 0, 0)
    send_piece("down", 0, 0, 1)
    send_piece("across", 0, 0, 2)

    loads[0].wait()
    loads[1].wait()

    def sums(i, carry):
        a, b = carry
        at = pl.ds(pl.multiple_of(i * 128, 128), 128)
        a = a + jnp.sum(rows[0, at, :].astype(F32).reshape(16, 8, 256), axis=0)
        b = b + jnp.sum(cols[at, :].astype(F32).reshape(16, 8, 512), axis=0)
        return a, b

    a, b = lax.fori_loop(0, 16, sums, (jnp.zeros((8, 256), F32), jnp.zeros((8, 512), F32)))
    stat[0, :, 0:256] = a
    stat[0, :, 256:768] = b
    start(stat.at[0], stat.at[1], st_send.at[0], st_recv.at[0], partner)
    arrived(stat.at[1], st_recv.at[0])
    stat[2] = stat[0] + stat[1]
    for k in range(3):
        start(stat.at[2], stat_x.at[k], st_send.at[1 + k], st_recv.at[1 + k], xs[k])
    for k in range(3):
        arrived(stat_x.at[k], st_recv.at[1 + k])
    stat[3] = (stat[2] + stat_x[1]) + (stat_x[0] + stat_x[2])
    start(stat.at[3], stat.at[4], st_send.at[4], st_recv.at[4], far)
    send_piece("up", 0, 0, 1)
    send_piece("down", 0, 0, 0)
    send_piece("across", 0, 0, 3)
    arrived(stat.at[4], st_recv.at[4])
    mean = jnp.sum(stat[3] + stat[4], axis=0, keepdims=True) / total
    rmean[0, 0] = jnp.broadcast_to(mean[:, 0:256], (8, 256))
    start(rmean.at[0, 0], rmean.at[0, 1], rm_send.at[0], rm_recv.at[0], near)
    send_piece("up", 0, 0, 2)
    send_piece("down", 0, 0, 3)
    send_piece("across", 0, 0, 0)

    loads[2].wait()
    loads[3].wait()
    col_mean = mean[:, 256:768]

    def right(i, carry):
        at = pl.ds(pl.multiple_of(i * 128, 128), 128)
        d = (cols[at, :].astype(F32) - col_mean).astype(BF16)
        e = jnp.broadcast_to(en[pl.ds(i, 1), :], (128, 128)).T
        e = jnp.concatenate([e, e, e, e], axis=1)
        rhs[at, 0:512] = d
        rhs[at, 512:1024] = (e * d.astype(F32) + grads[at, :].astype(F32)).astype(BF16)
        return carry

    lax.fori_loop(0, 16, right, 0)

    def multiply(dy, dz, order=0, wait=False):
        slot = dy * 4 + dz
        bank = slot % 2
        m = rmean[dz, dy, 0:1, :]
        pacc[bank] = jnp.zeros((256, 1024), F32)

        def step(i, carry):
            i = lax.rem(i + order, 4)
            at = pl.ds(pl.multiple_of(i * PIECE, PIECE), PIECE)
            if wait:
                arrived(rows.at[slot, at], rs_recv.at[slot, i])
            d = (rows[slot, at, :].astype(F32) - m).astype(BF16).T
            for h in range(2):
                cut = slice(h * 512, h * 512 + 512)
                pacc[bank, :, cut] += jnp.dot(d, rhs[at, cut], preferred_element_type=F32)
            return carry

        lax.fori_loop(0, 4, step, 0)
        for r in range(2):
            core_out[slot, r * 64:r * 64 + 64, :] = pacc[
                bank, pl.ds(pl.multiple_of(r * 128 + (1 - c) * 64, 64), 64), :].astype(BF16)
        start(core_out.at[slot], core_in.at[slot], c_send.at[slot], c_recv.at[slot], partner)

    def x_copy(dy, dz):
        slot = dy * 4 + dz
        owner = (q + dz) % 4
        k = (x - owner + 3) % 4
        return pltpu.make_async_remote_copy(
            src_ref=x_out.at[slot], dst_ref=x_in.at[dy, k],
            send_sem=x_send.at[slot], recv_sem=x_recv.at[dy, k],
            device_id=(walker(owner, yh, c), p, q), device_id_type=MESH)

    def combine(dy, dz):
        slot = dy * 4 + dz
        bank = slot % 2
        owner = (q + dz) % 4
        arrived(core_in.at[slot], c_recv.at[slot])
        parts = [
            pacc[bank, pl.ds(pl.multiple_of(r * 128 + c * 64, 64), 64), :]
            + core_in[slot, r * 64:r * 64 + 64, :].astype(F32)
            for r in range(2)
        ]

        @pl.when(owner == x)
        def _():
            for r in range(2):
                x_acc[dy, r * 64:r * 64 + 64, :] = parts[r]

        @pl.when(owner != x)
        def _():
            for r in range(2):
                x_out[slot, r * 64:r * 64 + 64, :] = parts[r].astype(BF16)
            x_copy(dy, dz).start()

    def x_total(dy, half):
        at = pl.ds(pl.multiple_of(half * 64, 64), 64)
        got = [x_in[dy, k, at, :].astype(F32) for k in range(3)]
        return (x_acc[dy, at, :] + got[1]) + (got[0] + got[2])

    multiply(0, 0)
    arrived(rmean.at[0, 1], rm_recv.at[0])
    start(rmean.at[0], rmean.at[3], rm_send.at[1], rm_recv.at[1], up)
    start(rmean.at[0], rmean.at[1], rm_send.at[2], rm_recv.at[2], down)
    send_piece("up", 0, 0, 3)
    send_piece("down", 0, 0, 2)
    send_piece("across", 0, 0, 1)
    combine(0, 0)

    piece_in(0, 3, 0)
    send_piece("up", 0, 3, 0)
    send_piece("across", 0, 3, 0)
    piece_in(0, 1, 1)
    send_piece("down", 0, 1, 1)
    send_piece("across", 0, 1, 1)
    piece_in(0, 3, 1)
    send_piece("across", 0, 3, 1)
    piece_in(0, 1, 0)
    send_piece("across", 0, 1, 0)
    arrived(rmean.at[3], rm_recv.at[1])
    start(rmean.at[3], rmean.at[2], rm_send.at[3], rm_recv.at[3], up)
    arrived(rmean.at[1], rm_recv.at[2])
    piece_in(0, 3, 2)
    send_piece("up", 0, 3, 2)
    piece_in(0, 1, 3)
    send_piece("down", 0, 1, 3)
    piece_in(1, 0, 2)
    send_piece("up", 1, 0, 2)
    piece_in(1, 0, 3)
    send_piece("down", 1, 0, 3)
    send_piece("up", 1, 0, 3)
    send_piece("down", 1, 0, 2)

    piece_in(1, 0, 0)
    piece_in(1, 0, 1)
    multiply(1, 0)
    piece_in(0, 3, 3)
    multiply(0, 3)
    combine(1, 0)
    combine(0, 3)
    piece_in(0, 1, 2)
    multiply(0, 1)
    piece_in(0, 2, 0)
    send_piece("across", 0, 2, 0)
    piece_in(0, 2, 1)
    send_piece("across", 0, 2, 1)
    combine(0, 1)
    arrived(rmean.at[2], rm_recv.at[3])
    piece_in(0, 2, 2)
    piece_in(0, 2, 3)
    multiply(0, 2)
    combine(0, 2)

    piece_in(1, 3, 2)
    send_piece("up", 1, 3, 2)
    piece_in(1, 1, 3)
    send_piece("down", 1, 1, 3)
    piece_in(1, 3, 0)
    piece_in(1, 3, 1)
    piece_in(1, 3, 3)
    multiply(1, 3)
    combine(1, 3)
    piece_in(1, 1, 0)
    piece_in(1, 1, 1)
    piece_in(1, 1, 2)
    multiply(1, 1)
    combine(1, 1)

    for k in range(3):
        arrived(x_in.at[0, k], x_recv.at[0, k])
    y_keep[...] = x_total(0, yh)
    y_out[0] = x_total(0, 1 - yh).astype(BF16)
    start(y_out.at[0], y_in.at[0], y_send.at[0], y_recv.at[0], far)

    multiply(1, 2, order=2, wait=True)
    combine(1, 2)

    for k in range(3):
        arrived(x_in.at[1, k], x_recv.at[1, k])
    y_out[1] = x_total(1, yh).astype(BF16)
    start(y_out.at[1], y_in.at[1], y_send.at[1], y_recv.at[1], near)
    y_out[2] = x_total(1, 1 - yh).astype(BF16)
    start(y_out.at[2], y_in.at[2], y_send.at[2], y_recv.at[2], diag)

    scale = 1.0 / total
    mine = pl.ds(pl.multiple_of(p * 512, 512), 512)
    other = pl.ds(pl.multiple_of((1 - p) * 512, 512), 512)
    arrived(y_in.at[0], y_recv.at[0])
    for ref, cut in ((cor_ref, slice(0, 512)), (ham_ref, slice(512, 1024))):
        ref[:, mine] = (y_keep[:, cut] + y_in[0, :, cut].astype(F32)) * scale
    arrived(y_in.at[1], y_recv.at[1])
    arrived(y_in.at[2], y_recv.at[2])
    for ref, cut in ((cor_ref, slice(0, 512)), (ham_ref, slice(512, 1024))):
        ref[:, other] = (y_in[1, :, cut].astype(F32) + y_in[2, :, cut].astype(F32)) * scale

    for copy in started:
        copy.wait_send()
    for dy in range(2):
        for dz in range(4):
            @pl.when((q + dz) % 4 != x)
            def _(dy=dy, dz=dz):
                x_copy(dy, dz).wait_send()


def per_device(o_rows, o_cols, grad_energy, energy):
    total = energy.shape[0] * lax.axis_size("walker")
    dma = pltpu.SemaphoreType.DMA
    out = jax.ShapeDtypeStruct((64, 1024), F32)
    hbm = pl.BlockSpec(memory_space=pl.ANY)
    vmem = pl.BlockSpec(memory_space=pltpu.VMEM)
    return pl.pallas_call(
        functools.partial(kernel, total),
        out_shape=(out, out),
        in_specs=[hbm] * 4,
        out_specs=(vmem, vmem),
        scratch_shapes=[
            pltpu.VMEM((8, 2048, 256), BF16),
            pltpu.VMEM((2048, 512), BF16),
            pltpu.VMEM((2048, 512), BF16),
            pltpu.VMEM((16, 128), F32),
            pltpu.VMEM((2048, 1024), BF16),
            pltpu.VMEM((2, 256, 1024), F32),
            pltpu.VMEM((5, 8, 768), F32),
            pltpu.VMEM((3, 8, 768), F32),
            pltpu.VMEM((4, 2, 8, 256), F32),
            pltpu.VMEM((8, 128, 1024), BF16),
            pltpu.VMEM((8, 128, 1024), BF16),
            pltpu.VMEM((8, 128, 1024), BF16),
            pltpu.VMEM((2, 3, 128, 1024), BF16),
            pltpu.VMEM((2, 128, 1024), F32),
            pltpu.VMEM((3, 64, 1024), BF16),
            pltpu.VMEM((3, 64, 1024), BF16),
            pltpu.VMEM((64, 1024), F32),
            dma((4,)),
            dma((28,)), dma((8, 4)),
            dma((5,)), dma((5,)),
            dma((4,)), dma((4,)),
            dma((8,)), dma((8,)),
            dma((8,)), dma((2, 3)),
            dma((3,)), dma((3,)),
        ],
        compiler_params=pltpu.CompilerParams(
            collective_id=0, has_side_effects=True, vmem_limit_bytes=56 * 1024 * 1024),
    )(o_rows, o_cols, grad_energy, energy.reshape(16, 128))


def solution(mesh):
    in_specs = (
        P("walker", ("prow", "pcol")),
        P("walker", ("pcol", "prow")),
        P("walker", ("pcol", "prow")),
        P("walker"),
    )
    out_specs = (P(("prow", "walker"), "pcol"), P(("prow", "walker"), "pcol"))
    return jax.shard_map(
        per_device, mesh=mesh, in_specs=in_specs, out_specs=out_specs, check_vma=False
    )
```
